32 devices in a mesh: dp: 4 (over y, x), fsdp: 8 (over z, core).
Axes of the slice: x: 2, y: 2, z: 4, core: 2. Of those that a mesh axis runs over, the one named last changes fastest.
Arguments:
- activations: bfloat16 [4096, 4096], P('fsdp'), may hold values from -6 to 6
- cotangent: bfloat16 [4096, 14336], P('fsdp', 'dp'), may hold values from -6 to 6
- next_input: bfloat16 [4096, 4096], P('fsdp'), may hold values from -6 to 6
- next_weight: bfloat16 [4096, 14336], P('fsdp', 'dp'), may hold values from -0.09375 to 0.09375
- master: float32 [4096, 14336], P('fsdp', 'dp'), may hold values from -0.0625 to 0.0625
- first_moment: float32 [4096, 14336], P('fsdp', 'dp'), may hold values from -0.12 to 0.12
- second_moment: float32 [4096, 14336], P('fsdp', 'dp'), may hold values from 1e-05 to 0.0003
- token_counts: int32 [8], P('fsdp'), may hold values from 128 to 512, as said below
- peer_groups: int32 [4], replicated, may hold values from 0 to 3, as said below
Outputs:
- next_output: bfloat16 [4096, 14336], P('fsdp', 'dp')
- new_master: float32 [4096, 14336], P('fsdp', 'dp')
- new_first: float32 [4096, 14336], P('fsdp', 'dp')
- new_second: float32 [4096, 14336], P('fsdp', 'dp')
- copy_master: float32 [4096, 14336], P('fsdp', 'dp')
- copy_first: float32 [4096, 14336], P('fsdp', 'dp')
- copy_second: float32 [4096, 14336], P('fsdp', 'dp')
The draws below stay inside these ranges and needn't reach their ends.
Inputs may be any that keep to these rules, and one draw needn't show every extreme that they name: token_counts[k] is the number of live rows in block k of 512 rows; rows at or past it are padding. peer_groups[g] = (g + s) mod 4 for one s from 1 to 3, the same s for every g.
All inputs are finite; a program needn't handle non-finite values.
Results may differ from the reference program's by a relative error of at most 0.025.
Values may be sent and summed in bfloat16 or wider, within the bound.
A program may use at most 192 MiB of HBM per device.

```python
import math
import jax
import jax.numpy as jnp
from jax import lax

D = 8192
MODEL_WIN = 4096
HIDDEN_WIN = 14336
TOK_DEV = 512
TOKENS = 4096
N_DP = 4
N_FSDP = 8


def draw_token_counts(key, part):
    indices = jnp.arange(N_FSDP, dtype=jnp.int32)
    lowest = TOK_DEV // 4
    rising = lowest + (TOK_DEV - lowest) * indices // max(N_FSDP - 1, 1)
    jitter = jax.random.randint(jax.random.fold_in(key, 11), (N_FSDP,), 0, TOK_DEV // 8 + 1)
    counts = jnp.maximum(rising - jitter, lowest)
    return counts.at[N_FSDP - 1].set(TOK_DEV).astype(jnp.int32)


def draw_peer_groups(key, part):
    mixed = jax.random.fold_in(jax.random.fold_in(key, 29), 1)
    raw_value = jax.random.randint(mixed, (), 0, 1048576)
    shift_by = 1 + raw_value % (N_DP - 1)
    return ((jnp.arange(N_DP, dtype=jnp.int32) + shift_by) % N_DP).astype(jnp.int32)


def levels(stream_key, extent, cuts, smallest, top_value):
    gain, own = 1.0, jax.random.fold_in(stream_key, 6)
    for dim, blocks in cuts:
        heights = jnp.exp(jax.random.uniform(jax.random.fold_in(own, dim), (blocks,), jnp.float32, smallest / len(cuts), top_value / len(cuts)))
        gain = gain * jnp.repeat(heights, extent[dim] // blocks).reshape([-1 if axis == dim else 1 for axis in range(len(extent))])
    return gain


def centred(rng, dims, width, limit, pieces=(), held_as=jnp.bfloat16):
    array = width * jax.random.normal(rng, dims, jnp.float32)
    if pieces:
        array = array * levels(rng, dims, pieces, -0.22, 0.18)
    return jnp.clip(array, -limit, limit).astype(held_as)


def setup_inputs(seed: int = 0) -> dict:
    splits = jax.random.split(jax.random.key(seed), 10)
    return {
        "activations": centred(splits[0], (TOKENS, MODEL_WIN), 1.0, 6.0, ((0, 8),)),
        "cotangent": centred(splits[1], (TOKENS, HIDDEN_WIN), 1.0, 6.0, ((0, 8), (1, 4))),
        "next_input": centred(splits[2], (TOKENS, MODEL_WIN), 1.0, 6.0, ((0, 8),)),
        "next_weight": centred(splits[3], (MODEL_WIN, HIDDEN_WIN), MODEL_WIN ** -0.5, 0.09375, ((0, 8), (1, 4))),
        "master": centred(splits[4], (MODEL_WIN, HIDDEN_WIN), D ** -0.5, 0.0625, ((0, 8), (1, 4)), jnp.float32),
        "first_moment": centred(splits[5], (MODEL_WIN, HIDDEN_WIN), 0.02, 0.12, ((0, 8), (1, 4)), jnp.float32),
        "second_moment": jnp.clip(jnp.exp(math.log(0.0003) - 3.4011975 * jax.random.uniform(splits[6], (MODEL_WIN, HIDDEN_WIN), jnp.float32) ** levels(splits[6], (MODEL_WIN, HIDDEN_WIN), ((0, 8), (1, 4)), -0.2, 0.2)), 9.999999747378752e-06, 0.0003),
        "token_counts": draw_token_counts(jax.random.fold_in(splits[9], 71), 0),
        "peer_groups": draw_peer_groups(jax.random.fold_in(splits[9], 71), 0),
    }


beta_first = 0.9
beta_second = 0.95
epsilon = 1e-05
learn_rate = 0.00015
decay_rate = 0.1

def adam_update(master, first_moment, second_moment, gradient):
    new_first = beta_first * first_moment + (1.0 - beta_first) * gradient
    new_second = beta_second * second_moment + (1.0 - beta_second) * gradient * gradient
    new_master = master - learn_rate * (new_first / (jnp.sqrt(new_second) + epsilon) + decay_rate * master)
    return (new_master, new_first, new_second)

def reference(activations, cotangent, next_input, next_weight, master, first_moment, second_moment, token_counts, peer_groups):
    input_blocks = activations.reshape(N_FSDP, TOK_DEV, MODEL_WIN)
    positions = jnp.arange(TOK_DEV, dtype=jnp.int32)
    live_rows = positions[None, :] < token_counts[:, None]
    masked = jnp.where(live_rows[:, :, None], cotangent.reshape(N_FSDP, TOK_DEV, HIDDEN_WIN), jnp.zeros((), cotangent.dtype))

    def accumulate(running, operands):
        input_block, cotangent_block = operands
        product = lax.dot_general(input_block, cotangent_block, (((0,), (0,)), ((), ())), preferred_element_type=jnp.float32)
        rounded = lax.optimization_barrier(product.astype(jnp.bfloat16))
        return (running + rounded.astype(jnp.float32), None)
    grad_sum, ignored = lax.scan(accumulate, jnp.zeros((MODEL_WIN, HIDDEN_WIN), jnp.float32), (input_blocks, masked))
    token_total = jnp.sum(token_counts).astype(jnp.float32)
    gradient = grad_sum / token_total
    new_master, new_first, new_second = adam_update(master, first_moment, second_moment, gradient)
    source = jnp.zeros((N_DP,), jnp.int32).at[peer_groups].set(jnp.arange(N_DP, dtype=jnp.int32))

    def copy_of(state):
        blocks = state.reshape(MODEL_WIN, N_DP, HIDDEN_WIN // N_DP)
        return jnp.take(blocks, source, axis=1).reshape(MODEL_WIN, HIDDEN_WIN)
    next_output = jnp.dot(next_input, next_weight, preferred_element_type=jnp.float32).astype(jnp.bfloat16)
    return (next_output, new_master, new_first, new_second, copy_of(new_master), copy_of(new_first), copy_of(new_second))
```

```python
from functools import partial

import jax
import jax.numpy as jnp
from jax import lax
from jax.experimental.layout import Layout, with_layout_constraint
from jax.sharding import PartitionSpec as P

beta_first = 0.9
beta_second = 0.95
epsilon = 1e-05
learn_rate = 0.00015
decay_rate = 0.1


def from_behind(shard, axis, by):
    size = lax.axis_size(axis)
    return lax.ppermute(shard, axis, [(i, (i + by) % size) for i in range(size)])


def adam_update(master, first_moment, second_moment, gradient):
    new_first = beta_first * first_moment + (1.0 - beta_first) * gradient
    new_second = beta_second * second_moment + (1.0 - beta_second) * gradient * gradient
    new_master = master - learn_rate * (
        new_first / (jnp.sqrt(new_second) + epsilon) + decay_rate * master
    )
    return (new_master, new_first, new_second)


def to_peer(sender, offset, groups):
    branches = [partial(sender, distance) for distance in range(1, groups)]
    return lax.switch(jnp.clip(offset - 1, 0, groups - 2), branches)


def body(
    activations,
    cotangent,
    next_input,
    next_weight,
    master,
    first_moment,
    second_moment,
    token_counts,
    peer_groups,
):
    groups = lax.axis_size("dp")
    offset = peer_groups[0]
    own_count = token_counts[0]
    token_total = lax.psum(own_count, "fsdp")
    positions = lax.broadcasted_iota(jnp.int32, (cotangent.shape[0], 1), 0)
    masked = jnp.where(positions < own_count, cotangent, jnp.zeros((), cotangent.dtype))
    partial_sums = lax.dot_general(
        activations, masked, (((0,), (0,)), ((), ())), preferred_element_type=jnp.float32
    ).astype(jnp.bfloat16)
    partial_sums = with_layout_constraint(partial_sums, Layout((0, 1)))
    grad_sum = lax.psum_scatter(partial_sums, "fsdp", scatter_dimension=0, tiled=True)
    grad_sum, next_weight = lax.optimization_barrier((grad_sum, next_weight))
    grad_sum = grad_sum.astype(jnp.float32)
    gathered = lax.all_gather(next_weight, "fsdp", axis=0, tiled=True)
    gradient = grad_sum / token_total.astype(jnp.float32)
    new_master, new_first, new_second = adam_update(master, first_moment, second_moment, gradient)
    copies = to_peer(
        lambda distance: (
            from_behind(new_master.astype(jnp.bfloat16), "dp", distance).astype(new_master.dtype),
            from_behind(new_first.astype(jnp.bfloat16), "dp", distance).astype(new_first.dtype),
            from_behind(new_second.astype(jnp.bfloat16), "dp", distance).astype(new_second.dtype),
        ),
        offset,
        groups,
    )
    gathered, copies = lax.optimization_barrier((gathered, copies))
    forward = jnp.dot(next_input, gathered, preferred_element_type=jnp.float32)
    return (
        with_layout_constraint(forward.astype(jnp.bfloat16), Layout((0, 1))),
        new_master,
        new_first,
        new_second,
        copies[0],
        copies[1],
        copies[2],
    )


def solution(mesh):
    return jax.shard_map(
        body,
        mesh=mesh,
        in_specs=(
            P("fsdp", None),
            P("fsdp", "dp"),
            P("fsdp", None),
            P("fsdp", "dp"),
            P("fsdp", "dp"),
            P("fsdp", "dp"),
            P("fsdp", "dp"),
            P("fsdp"),
            P(),
        ),
        out_specs=(
            P("fsdp", "dp"),
            P("fsdp", "dp"),
            P("fsdp", "dp"),
            P("fsdp", "dp"),
            P("fsdp", "dp"),
            P("fsdp", "dp"),
            P("fsdp", "dp"),
        ),
        check_vma=False,
    )
```

```python
from functools import partial

import jax
import jax.numpy as jnp
from jax import lax
from jax.experimental import pallas as pl
from jax.experimental.layout import Layout, with_layout_constraint
from jax.experimental.pallas import tpu as pltpu
from jax.sharding import PartitionSpec as P

beta_first = 0.9
beta_second = 0.95
epsilon = 1e-05
learn_rate = 0.00015
decay_rate = 0.1

MESH = pl.DeviceIdType.MESH
WIDTH = 256
HOP = 2
PARTS = 8


def adam_update(master, first_moment, second_moment, gradient):
    new_first = beta_first * first_moment + (1.0 - beta_first) * gradient
    new_second = beta_second * second_moment + (1.0 - beta_second) * gradient * gradient
    new_master = master - learn_rate * (
        new_first / (jnp.sqrt(new_second) + epsilon) + decay_rate * master
    )
    return (new_master, new_first, new_second)


def kernel(
    chips, groups, chunks, distance,
    total, sums, weight, master, first, second,
    gathered, out_master, out_first, out_second, copies,
    paired, arrived, own, state, fresh, staged,
    pair_send, pair_recv, line_send, line_recv, gather_send, gather_recv,
    twin_send, twin_recv, copy_send, copy_recv, own_sem, state_sem, fresh_sem, keep_sem,
):
    g = lax.axis_index("dp")
    f = lax.axis_index("fsdp")
    z = f // 2
    core = f % 2
    rows = weight.shape[0]
    piece = rows // PARTS
    last = chips - 1
    finish = 1 + HOP * last
    twin = (g, z * 2 + 1 - core)
    right = (g, ((z + 1) % chips) * 2 + core)
    left = (g, ((z + chips - 1) % chips) * 2 + core)
    peer = ((g + distance) % groups, f)
    giver = ((g + groups - distance) % groups, f)

    def cols(c):
        return pl.ds(pl.multiple_of(c * WIDTH, WIDTH), WIDTH)

    def remote(src, dst, send, recv, device):
        return pltpu.make_async_remote_copy(
            src_ref=src, dst_ref=dst, send_sem=send, recv_sem=recv,
            device_id=device, device_id_type=MESH,
        )

    def pair_copy(c):
        return remote(sums.at[:, 1 - core, :, cols(c)], paired.at[c],
                      pair_send.at[c], pair_recv.at[c], twin)

    def own_load(c):
        return pltpu.make_async_copy(sums.at[:, core, :, cols(c)], own.at[c % 3], own_sem.at[c % 3])

    def line_copy(c, d, slot, device):
        return remote(paired.at[c, d], arrived.at[c, slot],
                      line_send.at[c, d], line_recv.at[c, slot], device)

    def first_gather(c, way, device):
        return remote(weight.at[:, cols(c)], gathered.at[z, core, :, cols(c)],
                      gather_send.at[c, chips if way else z], gather_recv.at[c, z], device)

    def gather_copy(c, o, device):
        part = gathered.at[o, core, :, cols(c)]
        return remote(part, part, gather_send.at[c, o], gather_recv.at[c, o], device)

    def first_twin(c):
        return remote(weight.at[:, cols(c)], gathered.at[z, core, :, cols(c)],
                      twin_send.at[c, z], twin_recv.at[c, z], twin)

    def twin_copy(c, o):
        part = gathered.at[o, core, :, cols(c)]
        return remote(part, part, twin_send.at[c, o], twin_recv.at[c, o], twin)

    def twin_arrival(c, o):
        part = gathered.at[o, 1 - core, :, cols(c)]
        return remote(part, part, twin_send.at[c, o], twin_recv.at[c, o], twin)

    def peer_copy(c):
        return remote(staged.at[c], copies.at[:, :, cols(c)], copy_send.at[c], copy_recv.at[c], peer)

    def state_loads(c):
        return [
            pltpu.make_async_copy(ref.at[:, cols(c)], state.at[c % 2, i], state_sem.at[c % 2, i])
            for i, ref in enumerate((master, first, second))
        ]

    def fresh_stores(c):
        return [
            pltpu.make_async_copy(fresh.at[c % 2, i], ref.at[:, cols(c)], fresh_sem.at[c % 2, i])
            for i, ref in enumerate((out_master, out_first, out_second))
        ]

    def add_into(c, d, ref):
        @pl.loop(0, PARTS)
        def _(i):
            part = pl.ds(pl.multiple_of(i * piece, piece), piece)
            total_part = paired[c, d, part, :].astype(jnp.float32) + ref[part, :].astype(jnp.float32)
            paired[c, d, part, :] = total_part.astype(jnp.bfloat16)

    barrier = pltpu.get_barrier_semaphore()

    greeted = (twin, peer, giver, left, right)
    for device in greeted:
        pl.semaphore_signal(barrier, inc=1, device_id=device, device_id_type=MESH)
    pl.semaphore_wait(barrier, len(greeted))

    keep = pltpu.make_async_copy(weight, gathered.at[z, core], keep_sem)
    keep.start()
    pair_copy(0).start()
    own_load(0).start()

    def within(c):
        return jnp.logical_and(c >= 0, c < chunks)

    @pl.loop(0, chunks + finish)
    def _(t):
        @pl.when(t + 1 < chunks)
        def _():
            pair_copy(t + 1).start()
            own_load(t + 1).start()

        @pl.when(t < chunks)
        def _():
            @pl.when(z < last)
            def _():
                first_gather(t, 0, right).start()

            @pl.when(z > 0)
            def _():
                first_gather(t, 1, left).start()

            first_twin(t).start()

        for o in range(chips):
            from_left = t - HOP * (z - o)
            from_right = t - HOP * (o - z)

            @pl.when(jnp.logical_and(z > o, within(from_left)))
            def _():
                gather_copy(from_left, o, left).wait_recv()

                @pl.when(z < last)
                def _():
                    gather_copy(from_left, o, right).start()

                twin_copy(from_left, o).start()

            @pl.when(jnp.logical_and(z < o, within(from_right)))
            def _():
                gather_copy(from_right, o, right).wait_recv()

                @pl.when(z > 0)
                def _():
                    gather_copy(from_right, o, left).start()

                twin_copy(from_right, o).start()

        joined = t - 1

        @pl.when(within(joined))
        def _():
            pair_copy(joined).wait_recv()
            own_load(joined).wait()
            for d in range(chips):
                add_into(joined, d, own.at[joined % 3, d])

        rightward = t - 1 - HOP * z

        @pl.when(within(rightward))
        def _():
            for d in range(chips):
                @pl.when(z <= d)
                def _():
                    @pl.when(z > 0)
                    def _():
                        line_copy(rightward, d, d, left).wait_recv()
                        add_into(rightward, d, arrived.at[rightward, d])

                    @pl.when(z < d)
                    def _():
                        line_copy(rightward, d, d, right).start()

        leftward = t - 1 - HOP * (last - z)

        @pl.when(within(leftward))
        def _():
            for d in range(chips):
                @pl.when(z >= d)
                def _():
                    @pl.when(z < last)
                    def _():
                        @pl.when(z > d)
                        def _():
                            line_copy(leftward, d, d, right).wait_recv()
                            add_into(leftward, d, arrived.at[leftward, d])

                        @pl.when(z == d)
                        def _():
                            line_copy(leftward, d, chips, right).wait_recv()
                            add_into(leftward, d, arrived.at[leftward, chips])

                    @pl.when(z == d + 1)
                    def _():
                        line_copy(leftward, d, chips, left).start()

                    @pl.when(z > d + 1)
                    def _():
                        line_copy(leftward, d, d, left).start()

        coming = t + 1 - finish

        @pl.when(within(coming))
        def _():
            for copy in state_loads(coming):
                copy.start()

        done = t - finish

        @pl.when(within(done))
        def _():
            for copy in state_loads(done):
                copy.wait()

            @pl.when(done >= 2)
            def _():
                for copy in fresh_stores(done - 2):
                    copy.wait()

            slot = done % 2

            @pl.loop(0, PARTS)
            def _(i):
                part = pl.ds(pl.multiple_of(i * piece, piece), piece)
                gradient = paired[done, z, part, :].astype(jnp.float32) / total[0]
                results = adam_update(
                    state[slot, 0, part, :], state[slot, 1, part, :], state[slot, 2, part, :], gradient
                )
                for k, value in enumerate(results):
                    fresh[slot, k, part, :] = value
                    staged[done, k, part, :] = value.astype(jnp.bfloat16)

            peer_copy(done).start()
            for copy in fresh_stores(done):
                copy.start()

    keep.wait()
    for c in range(max(chunks - 2, 0), chunks):
        for copy in fresh_stores(c):
            copy.wait()

    @pl.loop(0, chunks)
    def _(c):
        pair_copy(c).wait_send()
        peer_copy(c).wait()
        first_twin(c).wait_send()

        @pl.when(z < last)
        def _():
            first_gather(c, 0, right).wait_send()

        @pl.when(z > 0)
        def _():
            first_gather(c, 1, left).wait_send()

        for o in range(chips):
            twin_arrival(c, o).wait_recv()

            @pl.when(z != o)
            def _():
                twin_copy(c, o).wait_send()
                line_copy(c, o, o, right).wait_send()

            @pl.when(jnp.logical_and(z > o, z < last))
            def _():
                gather_copy(c, o, right).wait_send()

            @pl.when(jnp.logical_and(z < o, z > 0))
            def _():
                gather_copy(c, o, left).wait_send()


def exchange(distance, total, sums, weight, master, first, second):
    groups, members = lax.axis_size("dp"), lax.axis_size("fsdp")
    rows, columns = weight.shape
    chips, chunks = members // 2, columns // WIDTH
    whole = pl.BlockSpec(memory_space=pl.ANY)
    dma = pltpu.SemaphoreType.DMA
    block = (rows, WIDTH)
    gathered, new_master, new_first, new_second, copies = pl.pallas_call(
        partial(kernel, chips, groups, chunks, distance),
        out_shape=(
            jax.ShapeDtypeStruct((chips, 2, rows, columns), weight.dtype),
            jax.ShapeDtypeStruct(master.shape, master.dtype),
            jax.ShapeDtypeStruct(first.shape, first.dtype),
            jax.ShapeDtypeStruct(second.shape, second.dtype),
            jax.ShapeDtypeStruct((3, rows, columns), jnp.bfloat16),
        ),
        in_specs=[pl.BlockSpec(memory_space=pltpu.SMEM)] + [whole] * 5,
        out_specs=(whole,) * 5,
        scratch_shapes=[
            pltpu.VMEM((chunks, chips) + block, jnp.bfloat16),
            pltpu.VMEM((chunks, chips + 1) + block, jnp.bfloat16),
            pltpu.VMEM((3, chips) + block, jnp.bfloat16),
            pltpu.VMEM((2, 3) + block, jnp.float32),
            pltpu.VMEM((2, 3) + block, jnp.float32),
            pltpu.VMEM((chunks, 3) + block, jnp.bfloat16),
            dma((chunks,)), dma((chunks,)),
            dma((chunks, chips)), dma((chunks, chips + 1)),
            dma((chunks, chips + 1)), dma((chunks, chips)),
            dma((chunks, chips)), dma((chunks, chips)),
            dma((chunks,)), dma((chunks,)),
            dma((3,)), dma((2, 3)), dma((2, 3)), dma(()),
        ],
        compiler_params=pltpu.CompilerParams(
            collective_id=distance, has_side_effects=True, vmem_limit_bytes=60 * 1024 * 1024
        ),
        name=f"exchange_{distance}",
    )(total, sums, weight, master, first, second)
    return (
        gathered, new_master, new_first, new_second,
        *(copies[i].astype(jnp.float32) for i in range(3)),
    )


def body(
    activations,
    cotangent,
    next_input,
    next_weight,
    master,
    first_moment,
    second_moment,
    token_counts,
    peer_groups,
):
    groups, members = lax.axis_size("dp"), lax.axis_size("fsdp")
    rows, columns = next_weight.shape
    own_count = token_counts[0]
    token_total = lax.psum(own_count, "fsdp").astype(jnp.float32).reshape(1)
    positions = lax.broadcasted_iota(jnp.int32, (cotangent.shape[0], 1), 0)
    masked = jnp.where(positions < own_count, cotangent, jnp.zeros((), cotangent.dtype))
    sums = lax.dot_general(
        activations, masked, (((0,), (0,)), ((), ())), preferred_element_type=jnp.float32
    ).astype(jnp.bfloat16)
    sums = with_layout_constraint(sums, Layout((0, 1))).reshape(members // 2, 2, rows, columns)
    branches = [partial(exchange, distance) for distance in range(1, groups)]
    gathered, *states = lax.switch(
        jnp.clip(peer_groups[0] - 1, 0, groups - 2), branches,
        token_total, sums, next_weight, master, first_moment, second_moment,
    )
    forward = jnp.dot(
        next_input, gathered.reshape(members * rows, columns), preferred_element_type=jnp.float32
    ).astype(jnp.bfloat16)
    return (with_layout_constraint(forward, Layout((0, 1))), *states)


def solution(mesh):
    return jax.shard_map(
        body,
        mesh=mesh,
        in_specs=(
            P("fsdp", None),
            P("fsdp", "dp"),
            P("fsdp", None),
            P("fsdp", "dp"),
            P("fsdp", "dp"),
            P("fsdp", "dp"),
            P("fsdp", "dp"),
            P("fsdp"),
            P(),
        ),
        out_specs=(P("fsdp", "dp"),) * 7,
        check_vma=False,
    )
```

```python
from functools import partial

import jax
import jax.numpy as jnp
from jax import lax
from jax.experimental import pallas as pl
from jax.experimental.layout import Layout, with_layout_constraint
from jax.experimental.pallas import tpu as pltpu
from jax.sharding import PartitionSpec as P

beta_first = 0.9
beta_second = 0.95
epsilon = 1e-05
learn_rate = 0.00015
decay_rate = 0.1

MESH = pl.DeviceIdType.MESH
WIDTH = 128
HOP = 2
PARTS = 8


def adam_update(master, first_moment, second_moment, gradient):
    new_first = beta_first * first_moment + (1.0 - beta_first) * gradient
    new_second = beta_second * second_moment + (1.0 - beta_second) * gradient * gradient
    new_master = master - learn_rate * (
        new_first / (jnp.sqrt(new_second) + epsilon) + decay_rate * master
    )
    return (new_master, new_first, new_second)


def kernel(
    chips, groups, chunks, distance,
    total, sums, weight, master, first, second,
    gathered, out_master, out_first, out_second, copies,
    paired, arrived, own, state, fresh, staged,
    pair_send, pair_recv, line_send, line_recv, gather_send, gather_recv,
    twin_send, twin_recv, copy_send, copy_recv, own_sem, state_sem, fresh_sem, keep_sem,
):
    g = lax.axis_index("dp")
    f = lax.axis_index("fsdp")
    z = f // 2
    core = f % 2
    rows = weight.shape[0]
    piece = rows // PARTS
    last = chips - 1
    finish = 1 + HOP * last
    twin = (g, z * 2 + 1 - core)
    right = (g, ((z + 1) % chips) * 2 + core)
    left = (g, ((z + chips - 1) % chips) * 2 + core)
    peer = ((g + distance) % groups, f)
    giver = ((g + groups - distance) % groups, f)

    def cols(c):
        return pl.ds(pl.multiple_of(c * WIDTH, WIDTH), WIDTH)

    def remote(src, dst, send, recv, device):
        return pltpu.make_async_remote_copy(
            src_ref=src, dst_ref=dst, send_sem=send, recv_sem=recv,
            device_id=device, device_id_type=MESH,
        )

    def pair_copy(c):
        return remote(sums.at[:, 1 - core, :, cols(c)], paired.at[c],
                      pair_send.at[c], pair_recv.at[c], twin)

    def own_load(c):
        return pltpu.make_async_copy(sums.at[:, core, :, cols(c)], own.at[c % 3], own_sem.at[c % 3])

    def line_copy(c, d, slot, device):
        return remote(paired.at[c, d], arrived.at[c, slot],
                      line_send.at[c, d], line_recv.at[c, slot], device)

    def first_gather(c, way, device):
        return remote(weight.at[:, cols(c)], gathered.at[z, core, :, cols(c)],
                      gather_send.at[c, chips if way else z], gather_recv.at[c, z], device)

    def gather_copy(c, o, device):
        part = gathered.at[o, core, :, cols(c)]
        return remote(part, part, gather_send.at[c, o], gather_recv.at[c, o], device)

    def first_twin(c):
        return remote(weight.at[:, cols(c)], gathered.at[z, core, :, cols(c)],
                      twin_send.at[c, z], twin_recv.at[c, z], twin)

    def twin_copy(c, o):
        part = gathered.at[o, core, :, cols(c)]
        return remote(part, part, twin_send.at[c, o], twin_recv.at[c, o], twin)

    def twin_arrival(c, o):
        part = gathered.at[o, 1 - core, :, cols(c)]
        return remote(part, part, twin_send.at[c, o], twin_recv.at[c, o], twin)

    def peer_copy(c):
        return remote(staged.at[c], copies.at[:, :, cols(c)], copy_send.at[c], copy_recv.at[c], peer)

    def state_loads(c):
        return [
            pltpu.make_async_copy(ref.at[:, cols(c)], state.at[c % 2, i], state_sem.at[c % 2, i])
            for i, ref in enumerate((master, first, second))
        ]

    def fresh_stores(c):
        return [
            pltpu.make_async_copy(fresh.at[c % 2, i], ref.at[:, cols(c)], fresh_sem.at[c % 2, i])
            for i, ref in enumerate((out_master, out_first, out_second))
        ]

    def add_into(c, d, ref):
        @pl.loop(0, PARTS)
        def _(i):
            part = pl.ds(pl.multiple_of(i * piece, piece), piece)
            total_part = paired[c, d, part, :].astype(jnp.float32) + ref[part, :].astype(jnp.float32)
            paired[c, d, part, :] = total_part.astype(jnp.bfloat16)

    barrier = pltpu.get_barrier_semaphore()

    greeted = (twin, peer, giver, left, right)
    for device in greeted:
        pl.semaphore_signal(barrier, inc=1, device_id=device, device_id_type=MESH)
    pl.semaphore_wait(barrier, len(greeted))

    keep = pltpu.make_async_copy(weight, gathered.at[z, core], keep_sem)
    keep.start()
    pair_copy(0).start()
    own_load(0).start()

    def within(c):
        return jnp.logical_and(c >= 0, c < chunks)

    @pl.loop(0, chunks + finish)
    def _(t):
        @pl.when(t + 1 < chunks)
        def _():
            pair_copy(t + 1).start()
            own_load(t + 1).start()

        @pl.when(t < chunks)
        def _():
            @pl.when(z < last)
            def _():
                first_gather(t, 0, right).start()

            @pl.when(z > 0)
            def _():
                first_gather(t, 1, left).start()

            first_twin(t).start()

        for o in range(chips):
            from_left = t - HOP * (z - o)
            from_right = t - HOP * (o - z)

            @pl.when(jnp.logical_and(z > o, within(from_left)))
            def _():
                gather_copy(from_left, o, left).wait_recv()

                @pl.when(z < last)
                def _():
                    gather_copy(from_left, o, right).start()

                twin_copy(from_left, o).start()

            @pl.when(jnp.logical_and(z < o, within(from_right)))
            def _():
                gather_copy(from_right, o, right).wait_recv()

                @pl.when(z > 0)
                def _():
                    gather_copy(from_right, o, left).start()

                twin_copy(from_right, o).start()

        joined = t - 1

        @pl.when(within(joined))
        def _():
            pair_copy(joined).wait_recv()
            own_load(joined).wait()
            for d in range(chips):
                add_into(joined, d, own.at[joined % 3, d])

        rightward = t - 1 - HOP * z

        @pl.when(within(rightward))
        def _():
            for d in range(chips):
                @pl.when(z <= d)
                def _():
                    @pl.when(z > 0)
                    def _():
                        line_copy(rightward, d, d, left).wait_recv()
                        add_into(rightward, d, arrived.at[rightward, d])

                    @pl.when(z < d)
                    def _():
                        line_copy(rightward, d, d, right).start()

        leftward = t - 1 - HOP * (last - z)

        @pl.when(within(leftward))
        def _():
            for d in range(chips):
                @pl.when(z >= d)
                def _():
                    @pl.when(z < last)
                    def _():
                        @pl.when(z > d)
                        def _():
                            line_copy(leftward, d, d, right).wait_recv()
                            add_into(leftward, d, arrived.at[leftward, d])

                        @pl.when(z == d)
                        def _():
                            line_copy(leftward, d, chips, right).wait_recv()
                            add_into(leftward, d, arrived.at[leftward, chips])

                    @pl.when(z == d + 1)
                    def _():
                        line_copy(leftward, d, chips, left).start()

                    @pl.when(z > d + 1)
                    def _():
                        line_copy(leftward, d, d, left).start()

        coming = t + 1 - finish

        @pl.when(within(coming))
        def _():
            for copy in state_loads(coming):
                copy.start()

        done = t - finish

        @pl.when(within(done))
        def _():
            for copy in state_loads(done):
                copy.wait()

            @pl.when(done >= 2)
            def _():
                for copy in fresh_stores(done - 2):
                    copy.wait()

            slot = done % 2

            @pl.loop(0, PARTS)
            def _(i):
                part = pl.ds(pl.multiple_of(i * piece, piece), piece)
                gradient = paired[done, z, part, :].astype(jnp.float32) / total[0]
                results = adam_update(
                    state[slot, 0, part, :], state[slot, 1, part, :], state[slot, 2, part, :], gradient
                )
                for k, value in enumerate(results):
                    fresh[slot, k, part, :] = value
                    staged[done, k, part, :] = value.astype(jnp.bfloat16)

            peer_copy(done).start()
            for copy in fresh_stores(done):
                copy.start()

    keep.wait()
    for c in range(max(chunks - 2, 0), chunks):
        for copy in fresh_stores(c):
            copy.wait()

    @pl.loop(0, chunks)
    def _(c):
        pair_copy(c).wait_send()
        peer_copy(c).wait()
        first_twin(c).wait_send()

        @pl.when(z < last)
        def _():
            first_gather(c, 0, right).wait_send()

        @pl.when(z > 0)
        def _():
            first_gather(c, 1, left).wait_send()

        for o in range(chips):
            twin_arrival(c, o).wait_recv()

            @pl.when(z != o)
            def _():
                twin_copy(c, o).wait_send()
                line_copy(c, o, o, right).wait_send()

            @pl.when(jnp.logical_and(z > o, z < last))
            def _():
                gather_copy(c, o, right).wait_send()

            @pl.when(jnp.logical_and(z < o, z > 0))
            def _():
                gather_copy(c, o, left).wait_send()


def exchange(distance, total, sums, weight, master, first, second):
    groups, members = lax.axis_size("dp"), lax.axis_size("fsdp")
    rows, columns = weight.shape
    chips, chunks = members // 2, columns // WIDTH
    whole = pl.BlockSpec(memory_space=pl.ANY)
    dma = pltpu.SemaphoreType.DMA
    block = (rows, WIDTH)
    gathered, new_master, new_first, new_second, copies = pl.pallas_call(
        partial(kernel, chips, groups, chunks, distance),
        out_shape=(
            jax.ShapeDtypeStruct((chips, 2, rows, columns), weight.dtype),
            jax.ShapeDtypeStruct(master.shape, master.dtype),
            jax.ShapeDtypeStruct(first.shape, first.dtype),
            jax.ShapeDtypeStruct(second.shape, second.dtype),
            jax.ShapeDtypeStruct((3, rows, columns), jnp.bfloat16),
        ),
        in_specs=[pl.BlockSpec(memory_space=pltpu.SMEM)] + [whole] * 5,
        out_specs=(whole,) * 5,
        scratch_shapes=[
            pltpu.VMEM((chunks, chips) + block, jnp.bfloat16),
            pltpu.VMEM((chunks, chips + 1) + block, jnp.bfloat16),
            pltpu.VMEM((3, chips) + block, jnp.bfloat16),
            pltpu.VMEM((2, 3) + block, jnp.float32),
            pltpu.VMEM((2, 3) + block, jnp.float32),
            pltpu.VMEM((chunks, 3) + block, jnp.bfloat16),
            dma((chunks,)), dma((chunks,)),
            dma((chunks, chips)), dma((chunks, chips + 1)),
            dma((chunks, chips + 1)), dma((chunks, chips)),
            dma((chunks, chips)), dma((chunks, chips)),
            dma((chunks,)), dma((chunks,)),
            dma((3,)), dma((2, 3)), dma((2, 3)), dma(()),
        ],
        compiler_params=pltpu.CompilerParams(
            collective_id=distance, has_side_effects=True, vmem_limit_bytes=60 * 1024 * 1024
        ),
        name=f"exchange_{distance}",
    )(total, sums, weight, master, first, second)
    return (
        gathered, new_master, new_first, new_second,
        *(copies[i].astype(jnp.float32) for i in range(3)),
    )


def body(
    activations,
    cotangent,
    next_input,
    next_weight,
    master,
    first_moment,
    second_moment,
    token_counts,
    peer_groups,
):
    groups, members = lax.axis_size("dp"), lax.axis_size("fsdp")
    rows, columns = next_weight.shape
    own_count = token_counts[0]
    token_total = lax.psum(own_count, "fsdp").astype(jnp.float32).reshape(1)
    positions = lax.broadcasted_iota(jnp.int32, (cotangent.shape[0], 1), 0)
    masked = jnp.where(positions < own_count, cotangent, jnp.zeros((), cotangent.dtype))
    sums = lax.dot_general(
        activations, masked, (((0,), (0,)), ((), ())), preferred_element_type=jnp.float32
    ).astype(jnp.bfloat16)
    sums = with_layout_constraint(sums, Layout((0, 1))).reshape(members // 2, 2, rows, columns)
    branches = [partial(exchange, distance) for distance in range(1, groups)]
    gathered, *states = lax.switch(
        jnp.clip(peer_groups[0] - 1, 0, groups - 2), branches,
        token_total, sums, next_weight, master, first_moment, second_moment,
    )
    forward = jnp.dot(
        next_input, gathered.reshape(members * rows, columns), preferred_element_type=jnp.float32
    ).astype(jnp.bfloat16)
    return (with_layout_constraint(forward, Layout((0, 1))), *states)


def solution(mesh):
    return jax.shard_map(
        body,
        mesh=mesh,
        in_specs=(
            P("fsdp", None),
            P("fsdp", "dp"),
            P("fsdp", None),
            P("fsdp", "dp"),
            P("fsdp", "dp"),
            P("fsdp", "dp"),
            P("fsdp", "dp"),
            P("fsdp"),
            P(),
        ),
        out_specs=(P("fsdp", "dp"),) * 7,
        check_vma=False,
    )
```
